32 devices in a mesh: dp: 8 (over y, x, core), eshard: 4 (over z).
Axes of the slice: x: 2, y: 2, z: 4, core: 2. Of those that a mesh axis runs over, the one named last changes fastest.
Arguments:
- tokens: bfloat16 [2048, 4096], P('dp', 'eshard'), may hold values from -6 to 6
- cotangent: bfloat16 [2048, 4096], P('dp', 'eshard'), may hold values from -6 to 6
- route_ids: int32 [2048, 2], P('dp'), may hold values from 0 to 63, all different within a row; in each aligned block of 256 rows (0 to 255, 256 to 511, ...) at most 16 rows name the same one
- gate_fixed: int32 [2048, 2], P('dp'), may hold values from 1 to 65535
- w_gate: bfloat16 [4096, 32768], P('eshard', 'dp'), may hold values from -0.09375 to 0.09375
- w_up: bfloat16 [4096, 32768], P('eshard', 'dp'), may hold values from -0.09375 to 0.09375
- w_down: bfloat16 [32768, 4096], P('dp', 'eshard'), may hold values from -0.0625 to 0.0625
Outputs:
- mixed: bfloat16 [2048, 4096], P('dp', 'eshard')
- token_grad: bfloat16 [2048, 4096], P('dp', 'eshard')
- grad_w_gate: bfloat16 [4096, 32768], P('eshard', 'dp')
- grad_w_up: bfloat16 [4096, 32768], P('eshard', 'dp')
- grad_w_down: bfloat16 [32768, 4096], P('dp', 'eshard')
The draws below stay inside these ranges and needn't reach their ends.
Inputs may be any that keep to these rules, and one draw needn't show every extreme that they name: `route_ids`: the two ids of a token differ; among the 256 tokens of one index of dp, no id is named by more than 16 routes, a bound that some block reaches.
All inputs are finite; a program needn't handle non-finite values.
Results may differ from the reference program's by a relative error of at most 0.028.
Values may be sent and summed in bfloat16 or wider, within the bound.
A program may use at most 128 MiB of HBM per device.

```python
import math
import jax
import jax.numpy as jnp
import numpy as np
from jax import lax

D = 4096
HIDDEN_SIZE = 8192
ROUTED = 64
EXPERTS = 4
TOK_DEV = 256
CAP = 16
TOKENS = 2048
N_DP = 8
N_ESHARD = 4


def set_ends(drawn, rng, least, largest):
    longest = drawn.shape.index(max(drawn.shape))
    spots = []
    for shift in (0, 1):
        where = [jax.random.randint(jax.random.fold_in(rng, axis), (), 0, length) for axis, length in enumerate(drawn.shape)]
        where[longest] = (where[longest] + shift) % drawn.shape[longest]
        spots.append(tuple(where))
    return drawn.at[spots[0]].set(least).at[spots[1]].set(largest)


def block_levels(rng, dims, split, low, high):
    level = 1.0
    for position, parts in split:
        heights = jax.random.uniform(jax.random.fold_in(jax.random.fold_in(rng, 6), position), (parts,), jnp.float32, low / len(split), high / len(split))
        level = level * jnp.repeat(jnp.exp(heights), dims[position] // parts).reshape((-1,) + (1,) * (len(dims) - 1 - position))
    return level


def assign_block(rng, own, number, rows, number_of, top, reach, skew):
    ranking = jax.random.permutation(rng, number_of)
    packed, common = portions_of(number_of, rows * top, reach, skew, True), portions_of(number_of, rows * top, reach, skew, False)
    places = jnp.arange(number_of)

    def named(sizes, turn):
        used = int((sizes > 0).sum())
        fixed = max(1, used // 4)
        passed = fixed + (places - fixed + turn * (used - fixed)) % max(1, number_of - fixed)
        return jnp.zeros((number_of,), jnp.int32).at[ranking[jnp.where(places < fixed, places, passed)]].set(jnp.asarray(sizes, jnp.int32))

    sizes = jnp.where(number % 4 == 0, named(packed, number // 4), named(common, number - number // 4 - 1))
    mixed = jax.random.permutation(jax.random.fold_in(own, 3), number_of)
    giver, receiver = mixed[0:number_of // 2 * 2:2], mixed[1:number_of // 2 * 2:2]
    margin = jnp.minimum(sizes[giver] - 1, reach - sizes[receiver]) // 2
    margin = jnp.where((giver == ranking[0]) | (receiver == ranking[0]) | (sizes[receiver] == 0), 0, jnp.maximum(margin, 0))
    passed = jax.random.randint(jax.random.fold_in(own, 4), (number_of // 2,), 0, 1 << 20) % (margin + 1)
    sizes = sizes.at[giver].add(-passed).at[receiver].add(passed)
    labels = jnp.searchsorted(jnp.cumsum(sizes), jnp.arange(rows * top), side="right").astype(jnp.int32)
    table = labels.reshape(top, rows).T
    table = table[jax.random.permutation(jax.random.fold_in(own, 1), rows)]
    turn = jax.random.randint(jax.random.fold_in(own, 2), (rows, 1), 0, top)
    return jnp.take_along_axis(table, (jnp.arange(top)[None, :] + turn) % top, axis=1)


def portions_of(count, total, reach, slope, full):
    loads = [(1 << 20) // math.isqrt(grade ** slope) + 1 for grade in range(1, count + 1)]
    largest = reach if full else min(reach, max(-(-total // count), total * loads[0] // sum(loads)))
    least = 1 if total - largest >= count - 1 else 0
    given, rest = [largest] + [least] * (count - 1), total - largest - least * (count - 1)
    while rest > 0:
        movable = [i for i in range(1, count) if given[i] < largest] or [i for i in range(1, count) if given[i] < reach]
        pool, budget = sum([loads[i] for i in movable]), rest
        for i in movable:
            more = min(reach - given[i], max(1, budget * loads[i] // pool), rest)
            given[i] = given[i] + more
            rest = rest - more
    return np.array(given)


def scatter_about(rng, shape, deviation, bound, shards=(), held_as=jnp.bfloat16):
    drawn = deviation * jax.random.normal(rng, shape, jnp.float32)
    if shards:
        drawn = drawn * block_levels(rng, shape, shards, -0.22, 0.18)
    return jnp.clip(drawn, -bound, bound).astype(held_as)


def setup_inputs(seed: int = 0) -> dict:
    key_of = jax.random.split(jax.random.key(seed), 8)
    tokens = scatter_about(key_of[0], (TOKENS, D), 1.0, 6.0, ((0, 8), (1, 4)))
    cotangent = scatter_about(key_of[1], (TOKENS, D), 1.0, 6.0, ((0, 8), (1, 4)))
    route_ids_keys = jax.random.split(jax.random.fold_in(key_of[2], 1), TOKENS // TOK_DEV)
    route_ids_turns = jax.random.permutation(jax.random.fold_in(key_of[2], 3), TOKENS // TOK_DEV)
    route_ids = jax.vmap(lambda own, number: assign_block(jax.random.fold_in(key_of[2], 2), own, number, TOK_DEV, ROUTED, 2, CAP, 2))(route_ids_keys, route_ids_turns).reshape((TOKENS, 2))
    gate_fixed = set_ends(jax.random.randint(key_of[3], (TOKENS, 2), 1, 65536), jax.random.fold_in(key_of[3], 1), 1, 65535).astype(jnp.int32)
    w_gate = scatter_about(key_of[4], (D, EXPERTS * HIDDEN_SIZE), D ** -0.5, 0.09375, ((0, 4), (1, 8)))
    w_up = scatter_about(key_of[5], (D, EXPERTS * HIDDEN_SIZE), D ** -0.5, 0.09375, ((0, 4), (1, 8)))
    w_down = scatter_about(key_of[6], (EXPERTS * HIDDEN_SIZE, D), HIDDEN_SIZE ** -0.5, 0.0625, ((0, 8), (1, 4)))
    return {"tokens": tokens, "cotangent": cotangent, "route_ids": route_ids, "gate_fixed": gate_fixed, "w_gate": w_gate, "w_up": w_up, "w_down": w_down}


def routing(ids, gates):
    expert_ids = jnp.arange(EXPERTS, dtype=jnp.int32)
    hits = (ids[:, :, None] == expert_ids[None, None, :]).astype(jnp.int32)
    hit_tok = jnp.sum(hits, axis=1).astype(jnp.int32)
    gate_values = gates.astype(jnp.float32) / 65536.0
    weight_tok = jnp.sum(hits.astype(jnp.float32) * gate_values[:, :, None], axis=1)
    slots = (jnp.cumsum(hit_tok, axis=0) - hit_tok).astype(jnp.int32)
    target = expert_ids[None, :] * CAP + slots
    rows = jnp.arange(EXPERTS * CAP, dtype=jnp.int32)
    match = (target[None, :, :] == rows[:, None, None]).astype(jnp.float32) * hit_tok[None, :, :].astype(jnp.float32)
    select = jnp.sum(match, axis=2)
    weighted = jnp.sum(match * weight_tok[None, :, :], axis=2)
    return select, weighted


def block_sum(left, right, transpose_right):
    blocks = D // N_ESHARD
    total = None
    for piece in range(N_ESHARD):
        lhs = left[:, piece * blocks:(piece + 1) * blocks]
        if transpose_right:
            rhs = jnp.transpose(right[:, piece * blocks:(piece + 1) * blocks])
        else:
            rhs = right[piece * blocks:(piece + 1) * blocks, :]
        term = jnp.dot(lhs, rhs, preferred_element_type=jnp.float32).astype(jnp.bfloat16).astype(jnp.float32)
        total = term if total is None else total + term
    return total


def reference(tokens, cotangent, route_ids, gate_fixed, w_gate, w_up, w_down):
    ids = route_ids.reshape(N_DP, TOK_DEV, 2)
    gates = gate_fixed.reshape(N_DP, TOK_DEV, 2)
    select, weighted = jax.vmap(routing)(ids, gates)
    tok = tokens.reshape(N_DP, TOK_DEV, D).astype(jnp.float32)
    cot = cotangent.reshape(N_DP, TOK_DEV, D).astype(jnp.float32)
    hp = lax.Precision.HIGHEST
    x_rows = jnp.einsum('bit,btd->bid', select, tok, precision=hp).astype(jnp.bfloat16)
    g_rows = jnp.einsum('bit,btd->bid', weighted, cot, precision=hp).astype(jnp.bfloat16)
    x_rows = jnp.transpose(x_rows.reshape(N_DP, EXPERTS, CAP, D), (1, 0, 2, 3)).reshape(EXPERTS, N_DP * CAP, D)
    g_rows = jnp.transpose(g_rows.reshape(N_DP, EXPERTS, CAP, D), (1, 0, 2, 3)).reshape(EXPERTS, N_DP * CAP, D)
    outs_y = []
    outs_dx = []
    grads_gate = []
    grads_up = []
    grads_down = []
    for expert in range(EXPERTS):
        inputs = x_rows[expert]
        route_grad = g_rows[expert]
        wg = w_gate[:, expert * HIDDEN_SIZE:(expert + 1) * HIDDEN_SIZE]
        wu = w_up[:, expert * HIDDEN_SIZE:(expert + 1) * HIDDEN_SIZE]
        wd = w_down[expert * HIDDEN_SIZE:(expert + 1) * HIDDEN_SIZE, :]
        gate_pre = block_sum(inputs, wg, False)
        up_pre = block_sum(inputs, wu, False)
        logistic = jax.nn.sigmoid(gate_pre)
        activated = gate_pre * logistic
        hidden = (activated * up_pre).astype(jnp.bfloat16)
        outs_y.append(jnp.dot(hidden, wd, preferred_element_type=jnp.float32))
        grad_hidden = block_sum(route_grad, wd, True)
        gate_grad = (grad_hidden * up_pre * logistic * (1.0 + gate_pre * (1.0 - logistic))).astype(jnp.bfloat16)
        up_grad = (grad_hidden * activated).astype(jnp.bfloat16)
        grads_gate.append(jnp.dot(jnp.transpose(inputs), gate_grad, preferred_element_type=jnp.float32).astype(jnp.bfloat16))
        grads_up.append(jnp.dot(jnp.transpose(inputs), up_grad, preferred_element_type=jnp.float32).astype(jnp.bfloat16))
        grads_down.append(jnp.dot(jnp.transpose(hidden), route_grad, preferred_element_type=jnp.float32).astype(jnp.bfloat16))
        back = jnp.dot(gate_grad, jnp.transpose(wg), preferred_element_type=jnp.float32)
        back = back + jnp.dot(up_grad, jnp.transpose(wu), preferred_element_type=jnp.float32)
        outs_dx.append(back)
    expert_out = jnp.stack(outs_y).reshape(EXPERTS, N_DP, CAP, D)
    expert_out = jnp.transpose(expert_out, (1, 0, 2, 3)).reshape(N_DP, EXPERTS * CAP, D)
    back_rows = jnp.stack(outs_dx).reshape(EXPERTS, N_DP, CAP, D)
    back_rows = jnp.transpose(back_rows, (1, 0, 2, 3)).reshape(N_DP, EXPERTS * CAP, D)
    mixed = jnp.einsum('bit,bid->btd', weighted, expert_out, precision=hp).reshape(TOKENS, D).astype(jnp.bfloat16)
    token_grad = jnp.einsum('bit,bid->btd', select, back_rows, precision=hp).reshape(TOKENS, D).astype(jnp.bfloat16)
    grad_w_gate = jnp.concatenate(grads_gate, axis=1)
    grad_w_up = jnp.concatenate(grads_up, axis=1)
    grad_w_down = jnp.concatenate(grads_down, axis=0)
    return (mixed, token_grad, grad_w_gate, grad_w_up, grad_w_down)
```

```python
import functools

import jax
import jax.numpy as jnp
from jax import lax
from jax.experimental import pallas as pl
from jax.experimental.pallas import tpu as pltpu
from jax.sharding import PartitionSpec as P

EXPERTS = 4
CAP = 16
WIDTH = 256
VMEM_BYTES = 60 * 1024 * 1024


def routing(ids, gates):
    expert_ids = jnp.arange(EXPERTS, dtype=jnp.int32)
    hits = (ids[:, :, None] == expert_ids[None, None, :]).astype(jnp.int32)
    hit_tok = jnp.sum(hits, axis=1)
    gate_values = gates.astype(jnp.float32) / 65536.0
    weight_tok = jnp.sum(hits.astype(jnp.float32) * gate_values[:, :, None], axis=1)
    slots = jnp.cumsum(hit_tok, axis=0) - hit_tok
    target = expert_ids[None, :] * CAP + slots
    rows = jnp.arange(EXPERTS * CAP, dtype=jnp.int32)
    match = (target[None, :, :] == rows[:, None, None]).astype(jnp.float32) * hit_tok[
        None, :, :
    ].astype(jnp.float32)
    select = jnp.sum(match, axis=2)
    weighted = jnp.sum(match * weight_tok[None, :, :], axis=2)
    return (select, weighted)


MESH = pl.DeviceIdType.MESH


def contract_cols(left, right):
    return lax.dot_general(
        left, right, (((1,), (1,)), ((), ())), preferred_element_type=jnp.float32
    )


def contract_rows(left, right):
    return lax.dot_general(
        left, right, (((0,), (0,)), ((), ())), preferred_element_type=jnp.float32
    )


def window_kernel(
    size, groups, members, chunks, width,
    tok_ref, grd_ref, wg_ref, wu_ref, wd_ref,
    hid_ref, gg_ref, ug_ref, x_ref, g_ref, back_ref,
    wg_v, wu_v, wd_v, x_v, g_v, part, outer, inner, full, out_acc, back_acc, y_send, y_recv,
    w_sem, xs_sem, xr_sem, in_sem, outer_sem, inner_sem, out_sem, ys_sem, yr_sem,
):
    me, z = lax.axis_index("dp"), lax.axis_index("eshard")
    cap = tok_ref.shape[0] // EXPERTS
    feats = tok_ref.shape[1]
    rows = groups * cap
    half = size // 2
    left = z < half
    middle = jnp.logical_or(z == half - 1, z == half)
    tip = jnp.logical_or(z == 0, z == size - 1)
    inward = jnp.where(left, z + 1, z - 1)
    outward = jnp.where(tip, z, jnp.where(left, z - 1, z + 1))
    distance = jnp.where(left, half - 1 - z, z - half)

    def weight_copies(c):
        cols = pl.ds(pl.multiple_of(c * width, width), width)
        return (
            pltpu.make_async_copy(wg_ref.at[:, cols], wg_v.at[c], w_sem.at[c, 0]),
            pltpu.make_async_copy(wu_ref.at[:, cols], wu_v.at[c], w_sem.at[c, 1]),
            pltpu.make_async_copy(wd_ref.at[cols, :], wd_v.at[c], w_sem.at[c, 2]),
        )

    @pl.loop(0, chunks)
    def _(c):
        for copy in weight_copies(c):
            copy.start()

    barrier = pltpu.get_barrier_semaphore()

    @pl.loop(1, groups)
    def _(k):
        pl.semaphore_signal(
            barrier, inc=1, device_id={"dp": lax.rem(me + k, groups)}, device_id_type=MESH
        )

    pl.semaphore_signal(barrier, inc=1, device_id={"eshard": inward}, device_id_type=MESH)

    @pl.when(jnp.logical_not(tip))
    def _():
        pl.semaphore_signal(barrier, inc=1, device_id={"eshard": outward}, device_id_type=MESH)

    pl.semaphore_wait(barrier, groups + jnp.where(tip, 0, 1))

    def row_copy(src, dst, which, k):
        to = lax.rem(me + k, groups)
        first = pl.multiple_of((to // members) * cap, cap)
        return pltpu.make_async_remote_copy(
            src_ref=src.at[pl.ds(first, cap), :],
            dst_ref=dst.at[me],
            send_sem=xs_sem.at[which, k],
            recv_sem=xr_sem.at[which, k],
            device_id={"dp": to},
            device_id_type=MESH,
        )

    for which, (src, dst) in enumerate(((tok_ref, x_v), (grd_ref, g_v))):

        @pl.loop(1, groups)
        def _(k):
            row_copy(src, dst, which, k).start()

        own = pl.multiple_of((me // members) * cap, cap)
        dst[me] = src[pl.ds(own, cap), :]

    for which, (src, dst) in enumerate(((tok_ref, x_v), (grd_ref, g_v))):

        @pl.loop(1, groups)
        def _(k):
            row_copy(src, dst, which, k).wait()

    x_ref[...] = x_v[...].reshape(rows, feats)
    g_ref[...] = g_v[...].reshape(rows, feats)
    out_acc[...] = jnp.zeros_like(out_acc)
    back_acc[...] = jnp.zeros_like(back_acc)

    def to_outer(c, k):
        return pltpu.make_async_remote_copy(
            src_ref=part.at[c, k], dst_ref=outer.at[c, k],
            send_sem=in_sem.at[c, k], recv_sem=outer_sem.at[c, k],
            device_id={"eshard": inward}, device_id_type=MESH,
        )

    def to_partner(c, k):
        return pltpu.make_async_remote_copy(
            src_ref=part.at[c, k], dst_ref=inner.at[c, k],
            send_sem=in_sem.at[c, k], recv_sem=inner_sem.at[c, k],
            device_id={"eshard": inward}, device_id_type=MESH,
        )

    def sum_out(c, k):
        return pltpu.make_async_remote_copy(
            src_ref=full.at[c, k], dst_ref=inner.at[c, k],
            send_sem=out_sem.at[c, k], recv_sem=inner_sem.at[c, k],
            device_id={"eshard": outward}, device_id_type=MESH,
        )

    def pass_out(c, k):
        return pltpu.make_async_remote_copy(
            src_ref=inner.at[c, k], dst_ref=inner.at[c, k],
            send_sem=out_sem.at[c, k], recv_sem=inner_sem.at[c, k],
            device_id={"eshard": outward}, device_id_type=MESH,
        )

    def gather_in(c):
        for copy in weight_copies(c):
            copy.wait()
        for k in range(3):
            if k == 0:
                own = jnp.dot(x_ref[...], wg_v[c], preferred_element_type=jnp.float32)
            elif k == 1:
                own = jnp.dot(x_ref[...], wu_v[c], preferred_element_type=jnp.float32)
            else:
                own = contract_cols(g_ref[...], wd_v[c])

            @pl.when(tip)
            def _():
                part[c, k] = own.astype(jnp.bfloat16)

            @pl.when(jnp.logical_not(tip))
            def _():
                to_outer(c, k).wait_recv()
                part[c, k] = (own + outer[c, k].astype(jnp.float32)).astype(jnp.bfloat16)

            @pl.when(middle)
            def _():
                to_partner(c, k).start()

            @pl.when(jnp.logical_not(middle))
            def _():
                to_outer(c, k).start()

    def finish(c):
        for k in range(3):
            to_partner(c, k).wait_recv()

            @pl.when(middle)
            def _():
                full[c, k] = (
                    part[c, k].astype(jnp.float32) + inner[c, k].astype(jnp.float32)
                ).astype(jnp.bfloat16)

            @pl.when(jnp.logical_and(middle, jnp.logical_not(tip)))
            def _():
                sum_out(c, k).start()

            @pl.when(jnp.logical_not(jnp.logical_or(middle, tip)))
            def _():
                pass_out(c, k).start()

        def summed(k):
            mine = part[c, k].astype(jnp.float32)
            return inner[c, k].astype(jnp.float32) + jnp.where(middle, mine, jnp.zeros_like(mine))

        gate, up, down = summed(0), summed(1), summed(2)
        logistic = 1.0 / (1.0 + jnp.exp(-gate))
        silu = gate * logistic
        hidden = (silu * up).astype(jnp.bfloat16)
        gate_grad = (down * up * logistic * (1.0 + gate * (1.0 - logistic))).astype(jnp.bfloat16)
        up_grad = (down * silu).astype(jnp.bfloat16)
        cols = pl.ds(pl.multiple_of(c * width, width), width)
        hid_ref[:, cols] = hidden
        gg_ref[:, cols] = gate_grad
        ug_ref[:, cols] = up_grad
        out_acc[...] += jnp.dot(hidden, wd_v[c], preferred_element_type=jnp.float32)
        back_acc[...] += contract_cols(gate_grad, wg_v[c]) + contract_cols(up_grad, wu_v[c])

    lag = jnp.where(middle, 1, 1 + 4 * distance)

    @pl.loop(0, chunks + 1 + 4 * (half - 1))
    def _(t):
        @pl.when(t < chunks)
        def _():
            gather_in(t)

        @pl.when(jnp.logical_and(t >= lag, t - lag < chunks))
        def _():
            finish(t - lag)

    y_send[0] = out_acc[...].astype(jnp.bfloat16).reshape(groups, cap, feats)
    y_send[1] = back_acc[...].astype(jnp.bfloat16).reshape(groups, cap, feats)

    def return_copy(which, k):
        to = lax.rem(me + k, groups)
        return pltpu.make_async_remote_copy(
            src_ref=y_send.at[which, to], dst_ref=y_recv.at[which, me],
            send_sem=ys_sem.at[which, k], recv_sem=yr_sem.at[which, k],
            device_id={"dp": to}, device_id_type=MESH,
        )

    for which in range(2):

        @pl.loop(1, groups)
        def _(k):
            return_copy(which, k).start()

        y_recv[which, me] = y_send[which, me]

    @pl.loop(0, chunks)
    def _(c):
        for k in range(3):
            to_outer(c, k).wait_send()

            @pl.when(jnp.logical_not(tip))
            def _():
                sum_out(c, k).wait_send()

    for which in range(2):

        @pl.loop(1, groups)
        def _(k):
            return_copy(which, k).wait()

    back_ref[...] = y_recv[...]


def run_window(token_rows, scaled_rows, w_gate, w_up, w_down):
    groups, size = lax.axis_size("dp"), lax.axis_size("eshard")
    members = groups // EXPERTS
    feats, hidden = w_gate.shape
    cap = token_rows.shape[0] // EXPERTS
    rows = groups * cap
    width = min(WIDTH, hidden)
    chunks = hidden // width
    bf16, f32 = jnp.bfloat16, jnp.float32
    vmem, hbm = pl.BlockSpec(memory_space=pltpu.VMEM), pl.BlockSpec(memory_space=pl.ANY)
    dma = pltpu.SemaphoreType.DMA
    wide = jax.ShapeDtypeStruct((rows, hidden), bf16)
    deep = jax.ShapeDtypeStruct((rows, feats), bf16)
    stage = pltpu.VMEM((chunks, 3, rows, width), bf16)
    return pl.pallas_call(
        functools.partial(window_kernel, size, groups, members, chunks, width),
        out_shape=(
            wide, wide, wide, deep, deep,
            jax.ShapeDtypeStruct((2, groups, cap, feats), bf16),
        ),
        in_specs=[vmem, vmem, hbm, hbm, hbm],
        out_specs=(vmem,) * 6,
        scratch_shapes=[
            pltpu.VMEM((chunks, feats, width), bf16),
            pltpu.VMEM((chunks, feats, width), bf16),
            pltpu.VMEM((chunks, width, feats), bf16),
            pltpu.VMEM((groups, cap, feats), bf16),
            pltpu.VMEM((groups, cap, feats), bf16),
            stage, stage, stage, stage,
            pltpu.VMEM((rows, feats), f32),
            pltpu.VMEM((rows, feats), f32),
            pltpu.VMEM((2, groups, cap, feats), bf16),
            pltpu.VMEM((2, groups, cap, feats), bf16),
            dma((chunks, 3)),
            dma((2, groups)), dma((2, groups)),
            dma((chunks, 3)), dma((chunks, 3)), dma((chunks, 3)), dma((chunks, 3)),
            dma((2, groups)), dma((2, groups)),
        ],
        compiler_params=pltpu.CompilerParams(
            collective_id=0, has_side_effects=True, vmem_limit_bytes=VMEM_BYTES
        ),
    )(token_rows, scaled_rows, w_gate, w_up, w_down)


def on_device(tokens, cotangent, route_ids, gate_fixed, w_gate, w_up, w_down):
    groups = lax.axis_size("dp")
    members = groups // EXPERTS
    features = tokens.shape[1]
    highest = lax.Precision.HIGHEST
    select, weighted = routing(route_ids, gate_fixed)
    capacity = select.shape[0] // EXPERTS
    token_rows = jnp.dot(
        select.astype(jnp.bfloat16), tokens, preferred_element_type=jnp.float32
    ).astype(jnp.bfloat16)
    scaled_rows = jnp.dot(weighted, cotangent.astype(jnp.float32), precision=highest).astype(
        jnp.bfloat16
    )
    hidden, gate_grad, up_grad, inputs, route_grad, returned = run_window(
        token_rows, scaled_rows, w_gate, w_up, w_down
    )
    grad_w_gate = contract_rows(inputs, gate_grad).astype(jnp.bfloat16)
    grad_w_up = contract_rows(inputs, up_grad).astype(jnp.bfloat16)
    grad_w_down = contract_rows(hidden, route_grad).astype(jnp.bfloat16)
    sums = jnp.sum(
        returned.astype(jnp.float32).reshape(2, EXPERTS, members, capacity, features), axis=2
    ).reshape(2, EXPERTS * capacity, features)
    mixed = jnp.dot(jnp.transpose(weighted), sums[0], precision=highest).astype(jnp.bfloat16)
    token_grad = jnp.dot(jnp.transpose(select), sums[1], precision=highest).astype(jnp.bfloat16)
    return (mixed, token_grad, grad_w_gate, grad_w_up, grad_w_down)


def solution(mesh):
    placed = (
        P("dp", "eshard"),
        P("dp", "eshard"),
        P("dp", None),
        P("dp", None),
        P("eshard", "dp"),
        P("eshard", "dp"),
        P("dp", "eshard"),
    )
    return jax.shard_map(
        on_device,
        mesh=mesh,
        in_specs=placed,
        out_specs=(
            P("dp", "eshard"),
            P("dp", "eshard"),
            P("eshard", "dp"),
            P("eshard", "dp"),
            P("dp", "eshard"),
        ),
        check_vma=False,
    )
```

```python
import functools

import jax
import jax.numpy as jnp
from jax import lax
from jax.experimental import pallas as pl
from jax.experimental.pallas import tpu as pltpu
from jax.sharding import PartitionSpec as P

EXPERTS = 4
CAP = 16
WIDTH = 256
VMEM_BYTES = 60 * 1024 * 1024


MESH = pl.DeviceIdType.MESH


def contract_cols(left, right):
    return lax.dot_general(
        left, right, (((1,), (1,)), ((), ())), preferred_element_type=jnp.float32
    )


def halves(value):
    high = value.astype(jnp.bfloat16)
    return high, (value - high.astype(jnp.float32)).astype(jnp.bfloat16)


def routing(ids, gates, cap):
    tokens = ids.shape[1]
    f32 = jnp.float32
    values = gates.astype(f32) * (1.0 / 65536.0)
    hits, weights = [], []
    for expert in range(EXPERTS):
        named = (ids == expert).astype(f32)
        hits.append(jnp.sum(named, axis=0, keepdims=True))
        weights.append(jnp.sum(named * values, axis=0, keepdims=True))
    hit = jnp.concatenate(hits, axis=0)
    earlier = (
        lax.broadcasted_iota(jnp.int32, (tokens, tokens), 0)
        < lax.broadcasted_iota(jnp.int32, (tokens, tokens), 1)
    ).astype(jnp.bfloat16)
    slots = jnp.dot(hit.astype(jnp.bfloat16), earlier, preferred_element_type=f32)
    places = lax.broadcasted_iota(jnp.int32, (cap, tokens), 0).astype(f32)
    select, weighted = [], []
    for expert in range(EXPERTS):
        here = (places == slots[expert : expert + 1]).astype(f32) * hits[expert]
        select.append(here)
        weighted.append(here * weights[expert])
    return jnp.concatenate(select, axis=0), jnp.concatenate(weighted, axis=0)


def window_kernel(
    size, groups, members, chunks, width,
    cap, ids_ref, gates_ref, tokens_ref, cot_ref, wg_ref, wu_ref, wd_ref,
    hid_ref, gg_ref, ug_ref, xt_ref, g_ref, back_ref, pick_ref,
    tok_ref, grd_ref, x_ref, wg_v, wu_v, wd_v, x_v, g_v, part, outer, inner, full, out_acc, back_acc, y_send, y_recv,
    w_sem, xs_sem, xr_sem, in_sem, outer_sem, inner_sem, out_sem, ys_sem, yr_sem,
):
    me, z = lax.axis_index("dp"), lax.axis_index("eshard")
    feats = tok_ref.shape[1]
    rows = groups * cap
    half = size // 2
    left = z < half
    middle = jnp.logical_or(z == half - 1, z == half)
    tip = jnp.logical_or(z == 0, z == size - 1)
    inward = jnp.where(left, z + 1, z - 1)
    outward = jnp.where(tip, z, jnp.where(left, z - 1, z + 1))
    distance = jnp.where(left, half - 1 - z, z - half)

    def weight_copies(c):
        cols = pl.ds(pl.multiple_of(c * width, width), width)
        return (
            pltpu.make_async_copy(wg_ref.at[:, cols], wg_v.at[c], w_sem.at[c, 0]),
            pltpu.make_async_copy(wu_ref.at[:, cols], wu_v.at[c], w_sem.at[c, 1]),
            pltpu.make_async_copy(wd_ref.at[cols, :], wd_v.at[c], w_sem.at[c, 2]),
        )

    @pl.loop(0, chunks)
    def _(c):
        for copy in weight_copies(c):
            copy.start()

    barrier = pltpu.get_barrier_semaphore()

    @pl.loop(1, groups)
    def _(k):
        pl.semaphore_signal(
            barrier, inc=1, device_id={"dp": lax.rem(me + k, groups)}, device_id_type=MESH
        )

    pl.semaphore_signal(barrier, inc=1, device_id={"eshard": inward}, device_id_type=MESH)

    @pl.when(jnp.logical_not(tip))
    def _():
        pl.semaphore_signal(barrier, inc=1, device_id={"eshard": outward}, device_id_type=MESH)

    select, weighted = routing(ids_ref[...], gates_ref[...], cap)
    tok_ref[...] = jnp.dot(
        select.astype(jnp.bfloat16), tokens_ref[...], preferred_element_type=jnp.float32
    ).astype(jnp.bfloat16)

    pl.semaphore_wait(barrier, groups + jnp.where(tip, 0, 1))

    def row_copy(src, dst, which, k):
        to = lax.rem(me + k, groups)
        first = pl.multiple_of((to // members) * cap, cap)
        return pltpu.make_async_remote_copy(
            src_ref=src.at[pl.ds(first, cap), :],
            dst_ref=dst.at[me],
            send_sem=xs_sem.at[which, k],
            recv_sem=xr_sem.at[which, k],
            device_id={"dp": to},
            device_id_type=MESH,
        )

    def send_rows(which, src, dst):
        @pl.loop(1, groups)
        def _(k):
            row_copy(src, dst, which, k).start()

        own = pl.multiple_of((me // members) * cap, cap)
        dst[me] = src[pl.ds(own, cap), :]

    def take_rows(which, src, dst):
        @pl.loop(1, groups)
        def _(k):
            row_copy(src, dst, which, k).wait()

    send_rows(0, tok_ref, x_v)
    high, low = halves(weighted)
    grd_ref[...] = (
        jnp.dot(high, cot_ref[...], preferred_element_type=jnp.float32)
        + jnp.dot(low, cot_ref[...], preferred_element_type=jnp.float32)
    ).astype(jnp.bfloat16)
    send_rows(1, grd_ref, g_v)
    pick_ref[0] = jnp.transpose(select).astype(jnp.bfloat16)
    high, low = halves(jnp.transpose(weighted))
    pick_ref[1] = high
    pick_ref[2] = low
    out_acc[...] = jnp.zeros_like(out_acc)
    back_acc[...] = jnp.zeros_like(back_acc)

    take_rows(0, tok_ref, x_v)
    x_ref[...] = x_v[...].reshape(rows, feats)

    def to_outer(c, k):
        return pltpu.make_async_remote_copy(
            src_ref=part.at[c, k], dst_ref=outer.at[c, k],
            send_sem=in_sem.at[c, k], recv_sem=outer_sem.at[c, k],
            device_id={"eshard": inward}, device_id_type=MESH,
        )

    def to_partner(c, k):
        return pltpu.make_async_remote_copy(
            src_ref=part.at[c, k], dst_ref=inner.at[c, k],
            send_sem=in_sem.at[c, k], recv_sem=inner_sem.at[c, k],
            device_id={"eshard": inward}, device_id_type=MESH,
        )

    def sum_out(c, k):
        return pltpu.make_async_remote_copy(
            src_ref=full.at[c, k], dst_ref=inner.at[c, k],
            send_sem=out_sem.at[c, k], recv_sem=inner_sem.at[c, k],
            device_id={"eshard": outward}, device_id_type=MESH,
        )

    def pass_out(c, k):
        return pltpu.make_async_remote_copy(
            src_ref=inner.at[c, k], dst_ref=inner.at[c, k],
            send_sem=out_sem.at[c, k], recv_sem=inner_sem.at[c, k],
            device_id={"eshard": outward}, device_id_type=MESH,
        )

    def gather_in(c):
        for copy in weight_copies(c):
            copy.wait()
        for k in range(3):
            if k == 0:
                own = jnp.dot(x_ref[...], wg_v[c], preferred_element_type=jnp.float32)
            elif k == 1:
                own = jnp.dot(x_ref[...], wu_v[c], preferred_element_type=jnp.float32)
            else:

                @pl.when(c == 0)
                def _():
                    take_rows(1, grd_ref, g_v)
                    g_ref[...] = g_v[...].reshape(rows, feats)

                own = contract_cols(g_ref[...], wd_v[c])

            @pl.when(tip)
            def _():
                part[c, k] = own.astype(jnp.bfloat16)

            @pl.when(jnp.logical_not(tip))
            def _():
                to_outer(c, k).wait_recv()
                part[c, k] = (own + outer[c, k].astype(jnp.float32)).astype(jnp.bfloat16)

            @pl.when(middle)
            def _():
                to_partner(c, k).start()

            @pl.when(jnp.logical_not(middle))
            def _():
                to_outer(c, k).start()

    def finish(c):
        for k in range(3):
            to_partner(c, k).wait_recv()

            @pl.when(middle)
            def _():
                full[c, k] = (
                    part[c, k].astype(jnp.float32) + inner[c, k].astype(jnp.float32)
                ).astype(jnp.bfloat16)

            @pl.when(jnp.logical_and(middle, jnp.logical_not(tip)))
            def _():
                sum_out(c, k).start()

            @pl.when(jnp.logical_not(jnp.logical_or(middle, tip)))
            def _():
                pass_out(c, k).start()

        def summed(k):
            mine = part[c, k].astype(jnp.float32)
            return inner[c, k].astype(jnp.float32) + jnp.where(middle, mine, jnp.zeros_like(mine))

        gate, up, down = summed(0), summed(1), summed(2)
        logistic = 1.0 / (1.0 + jnp.exp(-gate))
        silu = gate * logistic
        product = silu * up
        hidden = product.astype(jnp.bfloat16)
        gate_grad = (down * up * logistic * (1.0 + gate * (1.0 - logistic))).astype(jnp.bfloat16)
        up_grad = (down * silu).astype(jnp.bfloat16)
        cols = pl.ds(pl.multiple_of(c * width, width), width)
        hid_ref[cols, :] = jnp.transpose(product).astype(jnp.bfloat16)
        gg_ref[:, cols] = gate_grad
        ug_ref[:, cols] = up_grad
        out_acc[...] += jnp.dot(hidden, wd_v[c], preferred_element_type=jnp.float32)
        back_acc[...] += contract_cols(gate_grad, wg_v[c]) + contract_cols(up_grad, wu_v[c])

    lag = jnp.where(middle, 1, 1 + 4 * distance)

    @pl.loop(0, chunks + 1 + 4 * (half - 1))
    def _(t):
        @pl.when(t < chunks)
        def _():
            gather_in(t)

        @pl.when(jnp.logical_and(t >= lag, t - lag < chunks))
        def _():
            finish(t - lag)

        @pl.when(t == 1)
        def _():
            xt_ref[...] = jnp.transpose(x_ref[...].astype(jnp.float32)).astype(jnp.bfloat16)

    y_send[0] = out_acc[...].astype(jnp.bfloat16).reshape(groups, cap, feats)
    y_send[1] = back_acc[...].astype(jnp.bfloat16).reshape(groups, cap, feats)

    def return_copy(which, k):
        to = lax.rem(me + k, groups)
        return pltpu.make_async_remote_copy(
            src_ref=y_send.at[which, to], dst_ref=y_recv.at[which, me],
            send_sem=ys_sem.at[which, k], recv_sem=yr_sem.at[which, k],
            device_id={"dp": to}, device_id_type=MESH,
        )

    for which in range(2):

        @pl.loop(1, groups)
        def _(k):
            return_copy(which, k).start()

        y_recv[which, me] = y_send[which, me]

    @pl.loop(0, chunks)
    def _(c):
        for k in range(3):
            to_outer(c, k).wait_send()

            @pl.when(jnp.logical_not(tip))
            def _():
                sum_out(c, k).wait_send()

    for which in range(2):

        @pl.loop(1, groups)
        def _(k):
            return_copy(which, k).wait()

    back_ref[...] = y_recv[...]


def run_window(ids, gates, tokens, cotangent, w_gate, w_up, w_down):
    groups, size = lax.axis_size("dp"), lax.axis_size("eshard")
    members = groups // EXPERTS
    feats, hidden = w_gate.shape
    cap, count = CAP, tokens.shape[0]
    rows = groups * cap
    width = min(WIDTH, hidden)
    chunks = hidden // width
    bf16, f32 = jnp.bfloat16, jnp.float32
    vmem, hbm = pl.BlockSpec(memory_space=pltpu.VMEM), pl.BlockSpec(memory_space=pl.ANY)
    dma = pltpu.SemaphoreType.DMA
    wide = jax.ShapeDtypeStruct((rows, hidden), bf16)
    stage = pltpu.VMEM((chunks, 3, rows, width), bf16)
    return pl.pallas_call(
        functools.partial(window_kernel, size, groups, members, chunks, width, cap),
        out_shape=(
            jax.ShapeDtypeStruct((hidden, rows), bf16), wide, wide,
            jax.ShapeDtypeStruct((feats, rows), bf16),
            jax.ShapeDtypeStruct((rows, feats), bf16),
            jax.ShapeDtypeStruct((2, groups, cap, feats), bf16),
            jax.ShapeDtypeStruct((3, count, EXPERTS * cap), bf16),
        ),
        in_specs=[vmem, vmem, vmem, vmem, hbm, hbm, hbm],
        out_specs=(vmem,) * 7,
        scratch_shapes=[
            pltpu.VMEM((EXPERTS * cap, feats), bf16),
            pltpu.VMEM((EXPERTS * cap, feats), bf16),
            pltpu.VMEM((rows, feats), bf16),
            pltpu.VMEM((chunks, feats, width), bf16),
            pltpu.VMEM((chunks, feats, width), bf16),
            pltpu.VMEM((chunks, width, feats), bf16),
            pltpu.VMEM((groups, cap, feats), bf16),
            pltpu.VMEM((groups, cap, feats), bf16),
            stage, stage, stage, stage,
            pltpu.VMEM((rows, feats), f32),
            pltpu.VMEM((rows, feats), f32),
            pltpu.VMEM((2, groups, cap, feats), bf16),
            pltpu.VMEM((2, groups, cap, feats), bf16),
            dma((chunks, 3)),
            dma((2, groups)), dma((2, groups)),
            dma((chunks, 3)), dma((chunks, 3)), dma((chunks, 3)), dma((chunks, 3)),
            dma((2, groups)), dma((2, groups)),
        ],
        compiler_params=pltpu.CompilerParams(
            collective_id=0, has_side_effects=True, vmem_limit_bytes=VMEM_BYTES
        ),
    )(ids, gates, tokens, cotangent, w_gate, w_up, w_down)


def gradient_kernel(
    members, xt_ref, gg_ref, ug_ref, hid_ref, g_ref, back_ref, pick_ref,
    mixed_ref, token_ref, gate_ref, up_ref, down_ref,
):
    f32, bf16 = jnp.float32, jnp.bfloat16

    def product(left, right):
        return jnp.dot(left, right, preferred_element_type=f32)

    gate_ref[...] = product(xt_ref[...], gg_ref[...]).astype(bf16)
    up_ref[...] = product(xt_ref[...], ug_ref[...]).astype(bf16)
    down_ref[...] = product(hid_ref[...], g_ref[...]).astype(bf16)

    @pl.when(pl.program_id(0) == 0)
    def _():
        def gathered(which):
            parts = []
            for expert in range(EXPERTS):
                total = back_ref[which, expert * members].astype(f32)
                for member in range(1, members):
                    total = total + back_ref[which, expert * members + member].astype(f32)
                parts.append(total)
            return halves(jnp.concatenate(parts, axis=0))

        high, low = gathered(0)
        mixed_ref[...] = (
            product(pick_ref[1], high) + product(pick_ref[2], high) + product(pick_ref[1], low)
        ).astype(bf16)
        high, low = gathered(1)
        token_ref[...] = (product(pick_ref[0], high) + product(pick_ref[0], low)).astype(bf16)


def run_gradients(count, hidden_t, gate_grad, up_grad, inputs_t, route_grad, back, pick):
    groups = lax.axis_size("dp")
    feats, rows = inputs_t.shape
    hidden = hidden_t.shape[0]
    cap = back.shape[2]
    width = min(2 * WIDTH, hidden)
    bf16 = jnp.bfloat16

    def whole(shape):
        return pl.BlockSpec(shape, lambda i: (0,) * len(shape))

    across = pl.BlockSpec((rows, width), lambda i: (0, i))
    return pl.pallas_call(
        functools.partial(gradient_kernel, groups // EXPERTS),
        grid=(hidden // width,),
        out_shape=(
            jax.ShapeDtypeStruct((count, feats), bf16),
            jax.ShapeDtypeStruct((count, feats), bf16),
            jax.ShapeDtypeStruct((feats, hidden), bf16),
            jax.ShapeDtypeStruct((feats, hidden), bf16),
            jax.ShapeDtypeStruct((hidden, feats), bf16),
        ),
        in_specs=[
            whole((feats, rows)), across, across,
            pl.BlockSpec((width, rows), lambda i: (i, 0)),
            whole((rows, feats)), whole((2, groups, cap, feats)), whole(pick.shape),
        ],
        out_specs=(
            whole((count, feats)), whole((count, feats)),
            pl.BlockSpec((feats, width), lambda i: (0, i)),
            pl.BlockSpec((feats, width), lambda i: (0, i)),
            pl.BlockSpec((width, feats), lambda i: (i, 0)),
        ),
        compiler_params=pltpu.CompilerParams(vmem_limit_bytes=VMEM_BYTES),
    )(inputs_t, gate_grad, up_grad, hidden_t, route_grad, back, pick)


def on_device(tokens, cotangent, route_ids, gate_fixed, w_gate, w_up, w_down):
    hidden_t, gate_grad, up_grad, inputs_t, route_grad, back, pick = run_window(
        jnp.transpose(route_ids), jnp.transpose(gate_fixed), tokens, cotangent, w_gate, w_up, w_down
    )
    return run_gradients(
        tokens.shape[0], hidden_t, gate_grad, up_grad, inputs_t, route_grad, back, pick
    )


def solution(mesh):
    placed = (
        P("dp", "eshard"),
        P("dp", "eshard"),
        P("dp", None),
        P("dp", None),
        P("eshard", "dp"),
        P("eshard", "dp"),
        P("dp", "eshard"),
    )
    return jax.shard_map(
        on_device,
        mesh=mesh,
        in_specs=placed,
        out_specs=(
            P("dp", "eshard"),
            P("dp", "eshard"),
            P("eshard", "dp"),
            P("eshard", "dp"),
            P("dp", "eshard"),
        ),
        check_vma=False,
    )
```

```python
import functools

import jax
import jax.numpy as jnp
from jax import lax
from jax.experimental import pallas as pl
from jax.experimental.pallas import tpu as pltpu
from jax.sharding import PartitionSpec as P

EXPERTS = 4
CAP = 16
WIDTH = 256
VMEM_BYTES = 46 * 1024 * 1024
GRAD_BYTES = 24 * 1024 * 1024


MESH = pl.DeviceIdType.MESH


def contract_cols(left, right):
    return lax.dot_general(
        left, right, (((1,), (1,)), ((), ())), preferred_element_type=jnp.float32
    )


def halves(value):
    high = value.astype(jnp.bfloat16)
    return high, (value - high.astype(jnp.float32)).astype(jnp.bfloat16)


def routing(ids, gates, cap):
    tokens = ids.shape[1]
    f32 = jnp.float32
    values = gates.astype(f32) * (1.0 / 65536.0)
    hits, weights = [], []
    for expert in range(EXPERTS):
        named = (ids == expert).astype(f32)
        hits.append(jnp.sum(named, axis=0, keepdims=True))
        weights.append(jnp.sum(named * values, axis=0, keepdims=True))
    hit = jnp.concatenate(hits, axis=0)
    earlier = (
        lax.broadcasted_iota(jnp.int32, (tokens, tokens), 0)
        < lax.broadcasted_iota(jnp.int32, (tokens, tokens), 1)
    ).astype(jnp.bfloat16)
    slots = jnp.dot(hit.astype(jnp.bfloat16), earlier, preferred_element_type=f32)
    places = lax.broadcasted_iota(jnp.int32, (cap, tokens), 0).astype(f32)
    select, weighted = [], []
    for expert in range(EXPERTS):
        here = (places == slots[expert : expert + 1]).astype(f32) * hits[expert]
        select.append(here)
        weighted.append(here * weights[expert])
    return jnp.concatenate(select, axis=0), jnp.concatenate(weighted, axis=0)


def window_kernel(
    size, groups, members, chunks, width,
    cap, ids_ref, gates_ref, tokens_ref, cot_ref, wg_ref, wu_ref, wd_ref,
    hid_ref, gg_ref, ug_ref, xt_ref, g_ref, back_ref, pick_ref,
    tok_ref, grd_ref, x_ref, wg_v, wu_v, wd_v, x_v, g_v, part, outer, inner, full, out_acc, back_acc, y_send, y_recv,
    w_sem, xs_sem, xr_sem, in_sem, outer_sem, inner_sem, out_sem, ys_sem, yr_sem,
):
    me, z = lax.axis_index("dp"), lax.axis_index("eshard")
    feats = tok_ref.shape[1]
    rows = groups * cap
    half = size // 2
    left = z < half
    middle = jnp.logical_or(z == half - 1, z == half)
    tip = jnp.logical_or(z == 0, z == size - 1)
    inward = jnp.where(left, z + 1, z - 1)
    outward = jnp.where(tip, z, jnp.where(left, z - 1, z + 1))
    distance = jnp.where(left, half - 1 - z, z - half)

    def weight_copies(c):
        cols = pl.ds(pl.multiple_of(c * width, width), width)
        return (
            pltpu.make_async_copy(wg_ref.at[:, cols], wg_v.at[c], w_sem.at[c, 0]),
            pltpu.make_async_copy(wu_ref.at[:, cols], wu_v.at[c], w_sem.at[c, 1]),
            pltpu.make_async_copy(wd_ref.at[cols, :], wd_v.at[c], w_sem.at[c, 2]),
        )

    @pl.loop(0, chunks)
    def _(c):
        for copy in weight_copies(c):
            copy.start()

    barrier = pltpu.get_barrier_semaphore()

    @pl.loop(1, groups)
    def _(k):
        pl.semaphore_signal(
            barrier, inc=1, device_id={"dp": lax.rem(me + k, groups)}, device_id_type=MESH
        )

    pl.semaphore_signal(barrier, inc=1, device_id={"eshard": inward}, device_id_type=MESH)

    @pl.when(jnp.logical_not(tip))
    def _():
        pl.semaphore_signal(barrier, inc=1, device_id={"eshard": outward}, device_id_type=MESH)

    select, weighted = routing(ids_ref[...], gates_ref[...], cap)
    tok_ref[...] = jnp.dot(
        select.astype(jnp.bfloat16), tokens_ref[...], preferred_element_type=jnp.float32
    ).astype(jnp.bfloat16)

    pl.semaphore_wait(barrier, groups + jnp.where(tip, 0, 1))

    def row_copy(src, dst, which, k):
        to = lax.rem(me + k, groups)
        first = pl.multiple_of((to // members) * cap, cap)
        return pltpu.make_async_remote_copy(
            src_ref=src.at[pl.ds(first, cap), :],
            dst_ref=dst.at[me],
            send_sem=xs_sem.at[which, k],
            recv_sem=xr_sem.at[which, k],
            device_id={"dp": to},
            device_id_type=MESH,
        )

    def send_rows(which, src, dst):
        @pl.loop(1, groups)
        def _(k):
            row_copy(src, dst, which, k).start()

        own = pl.multiple_of((me // members) * cap, cap)
        dst[me] = src[pl.ds(own, cap), :]

    def take_rows(which, src, dst):
        @pl.loop(1, groups)
        def _(k):
            row_copy(src, dst, which, k).wait()

    send_rows(0, tok_ref, x_v)
    high, low = halves(weighted)
    grd_ref[...] = (
        jnp.dot(high, cot_ref[...], preferred_element_type=jnp.float32)
        + jnp.dot(low, cot_ref[...], preferred_element_type=jnp.float32)
    ).astype(jnp.bfloat16)
    send_rows(1, grd_ref, g_v)
    pick_ref[0] = jnp.transpose(select).astype(jnp.bfloat16)
    high, low = halves(jnp.transpose(weighted))
    pick_ref[1] = high
    pick_ref[2] = low
    out_acc[...] = jnp.zeros_like(out_acc)
    back_acc[...] = jnp.zeros_like(back_acc)

    take_rows(0, tok_ref, x_v)
    x_ref[...] = x_v[...].reshape(rows, feats)

    def to_outer(c, k):
        return pltpu.make_async_remote_copy(
            src_ref=part.at[c, k], dst_ref=outer.at[c, k],
            send_sem=in_sem.at[c, k], recv_sem=outer_sem.at[c, k],
            device_id={"eshard": inward}, device_id_type=MESH,
        )

    def to_partner(c, k):
        return pltpu.make_async_remote_copy(
            src_ref=part.at[c, k], dst_ref=inner.at[c, k],
            send_sem=in_sem.at[c, k], recv_sem=inner_sem.at[c, k],
            device_id={"eshard": inward}, device_id_type=MESH,
        )

    def sum_out(c, k):
        return pltpu.make_async_remote_copy(
            src_ref=full.at[c, k], dst_ref=inner.at[c, k],
            send_sem=out_sem.at[c, k], recv_sem=inner_sem.at[c, k],
            device_id={"eshard": outward}, device_id_type=MESH,
        )

    def pass_out(c, k):
        return pltpu.make_async_remote_copy(
            src_ref=inner.at[c, k], dst_ref=inner.at[c, k],
            send_sem=out_sem.at[c, k], recv_sem=inner_sem.at[c, k],
            device_id={"eshard": outward}, device_id_type=MESH,
        )

    def forward(c, k):
        to_partner(c, k).wait_recv()
        full[c, k] = (
            part[c, k].astype(jnp.float32) + inner[c, k].astype(jnp.float32)
        ).astype(jnp.bfloat16)

        @pl.when(jnp.logical_not(tip))
        def _():
            sum_out(c, k).start()

    def gather_in(c):
        for copy in weight_copies(c):
            copy.wait()
        for k in range(3):
            if k == 0:
                own = jnp.dot(x_ref[...], wg_v[c], preferred_element_type=jnp.float32)
            elif k == 1:
                own = jnp.dot(x_ref[...], wu_v[c], preferred_element_type=jnp.float32)
            else:

                @pl.when(c == 0)
                def _():
                    take_rows(1, grd_ref, g_v)
                    g_ref[...] = g_v[...].reshape(rows, feats)

                own = contract_cols(g_ref[...], wd_v[c])

            @pl.when(tip)
            def _():
                part[c, k] = own.astype(jnp.bfloat16)

            @pl.when(jnp.logical_not(tip))
            def _():
                to_outer(c, k).wait_recv()
                part[c, k] = (own + outer[c, k].astype(jnp.float32)).astype(jnp.bfloat16)

            @pl.when(middle)
            def _():
                to_partner(c, k).start()

            @pl.when(jnp.logical_not(middle))
            def _():
                to_outer(c, k).start()

            @pl.when(jnp.logical_and(middle, c > 0))
            def _():
                forward(c - 1, k)

    def return_copy(which, k):
        to = lax.rem(me + k, groups)
        return pltpu.make_async_remote_copy(
            src_ref=y_send.at[which, to], dst_ref=y_recv.at[which, me],
            send_sem=ys_sem.at[which, k], recv_sem=yr_sem.at[which, k],
            device_id={"dp": to}, device_id_type=MESH,
        )

    def send_home(which, total):
        y_send[which] = total[...].astype(jnp.bfloat16).reshape(groups, cap, feats)

        @pl.loop(1, groups)
        def _(k):
            return_copy(which, k).start()

        y_recv[which, me] = y_send[which, me]

    def finish(c):
        def summed(k):
            @pl.when(jnp.logical_not(middle))
            def _():
                to_partner(c, k).wait_recv()

            @pl.when(jnp.logical_not(jnp.logical_or(middle, tip)))
            def _():
                pass_out(c, k).start()

            @pl.when(jnp.logical_and(middle, c == chunks - 1))
            def _():
                forward(c, k)

            mine = part[c, k].astype(jnp.float32)
            return inner[c, k].astype(jnp.float32) + jnp.where(middle, mine, jnp.zeros_like(mine))

        gate, up = summed(0), summed(1)
        logistic = 1.0 / (1.0 + jnp.exp(-gate))
        silu = gate * logistic
        product = silu * up
        hidden = product.astype(jnp.bfloat16)
        cols = pl.ds(pl.multiple_of(c * width, width), width)
        out_acc[...] += jnp.dot(hidden, wd_v[c], preferred_element_type=jnp.float32)

        @pl.when(c == chunks - 1)
        def _():
            send_home(0, out_acc)

        down = summed(2)
        gate_grad = (down * up * logistic * (1.0 + gate * (1.0 - logistic))).astype(jnp.bfloat16)
        up_grad = (down * silu).astype(jnp.bfloat16)
        back_acc[...] += contract_cols(gate_grad, wg_v[c]) + contract_cols(up_grad, wu_v[c])

        @pl.when(c == chunks - 1)
        def _():
            send_home(1, back_acc)

        gg_ref[:, cols] = gate_grad
        ug_ref[:, cols] = up_grad
        hid_ref[cols, :] = jnp.transpose(product).astype(jnp.bfloat16)

    lag = jnp.where(middle, 1, 1 + 4 * distance)

    @pl.loop(0, chunks + 1 + 4 * (half - 1))
    def _(t):
        @pl.when(t < chunks)
        def _():
            gather_in(t)

        @pl.when(jnp.logical_and(t >= lag, t - lag < chunks))
        def _():
            finish(t - lag)

        @pl.when(t == 1)
        def _():
            xt_ref[...] = jnp.transpose(x_ref[...].astype(jnp.float32)).astype(jnp.bfloat16)

    @pl.loop(0, chunks)
    def _(c):
        for k in range(3):
            to_outer(c, k).wait_send()

            @pl.when(jnp.logical_not(tip))
            def _():
                sum_out(c, k).wait_send()

    for which in range(2):

        @pl.loop(1, groups)
        def _(k):
            return_copy(which, k).wait()

    back_ref[...] = y_recv[...]


def run_window(ids, gates, tokens, cotangent, w_gate, w_up, w_down):
    groups, size = lax.axis_size("dp"), lax.axis_size("eshard")
    members = groups // EXPERTS
    feats, hidden = w_gate.shape
    cap, count = CAP, tokens.shape[0]
    rows = groups * cap
    width = min(WIDTH, hidden)
    chunks = hidden // width
    bf16, f32 = jnp.bfloat16, jnp.float32
    vmem, hbm = pl.BlockSpec(memory_space=pltpu.VMEM), pl.BlockSpec(memory_space=pl.ANY)
    dma = pltpu.SemaphoreType.DMA
    wide = jax.ShapeDtypeStruct((rows, hidden), bf16)
    stage = pltpu.VMEM((chunks, 3, rows, width), bf16)
    return pl.pallas_call(
        functools.partial(window_kernel, size, groups, members, chunks, width, cap),
        out_shape=(
            jax.ShapeDtypeStruct((hidden, rows), bf16), wide, wide,
            jax.ShapeDtypeStruct((feats, rows), bf16),
            jax.ShapeDtypeStruct((rows, feats), bf16),
            jax.ShapeDtypeStruct((2, groups, cap, feats), bf16),
            jax.ShapeDtypeStruct((3, count, EXPERTS * cap), bf16),
        ),
        in_specs=[vmem, vmem, vmem, vmem, hbm, hbm, hbm],
        out_specs=(vmem,) * 7,
        scratch_shapes=[
            pltpu.VMEM((EXPERTS * cap, feats), bf16),
            pltpu.VMEM((EXPERTS * cap, feats), bf16),
            pltpu.VMEM((rows, feats), bf16),
            pltpu.VMEM((chunks, feats, width), bf16),
            pltpu.VMEM((chunks, feats, width), bf16),
            pltpu.VMEM((chunks, width, feats), bf16),
            pltpu.VMEM((groups, cap, feats), bf16),
            pltpu.VMEM((groups, cap, feats), bf16),
            stage, stage, stage, stage,
            pltpu.VMEM((rows, feats), f32),
            pltpu.VMEM((rows, feats), f32),
            pltpu.VMEM((2, groups, cap, feats), bf16),
            pltpu.VMEM((2, groups, cap, feats), bf16),
            dma((chunks, 3)),
            dma((2, groups)), dma((2, groups)),
            dma((chunks, 3)), dma((chunks, 3)), dma((chunks, 3)), dma((chunks, 3)),
            dma((2, groups)), dma((2, groups)),
        ],
        compiler_params=pltpu.CompilerParams(
            collective_id=0, has_side_effects=True, vmem_limit_bytes=VMEM_BYTES
        ),
    )(ids, gates, tokens, cotangent, w_gate, w_up, w_down)


def gradient_kernel(
    members, xt_ref, gg_ref, ug_ref, hid_ref, g_ref, back_ref, pick_ref,
    mixed_ref, token_ref, gate_ref, up_ref, down_ref,
):
    f32, bf16 = jnp.float32, jnp.bfloat16

    def product(left, right):
        return jnp.dot(left, right, preferred_element_type=f32)

    gate_ref[...] = product(xt_ref[...], gg_ref[...]).astype(bf16)
    up_ref[...] = product(xt_ref[...], ug_ref[...]).astype(bf16)
    down_ref[...] = product(hid_ref[...], g_ref[...]).astype(bf16)

    @pl.when(pl.program_id(0) == 0)
    def _():
        def gathered(which):
            parts = []
            for expert in range(EXPERTS):
                total = back_ref[which, expert * members].astype(f32)
                for member in range(1, members):
                    total = total + back_ref[which, expert * members + member].astype(f32)
                parts.append(total)
            return halves(jnp.concatenate(parts, axis=0))

        high, low = gathered(0)
        mixed_ref[...] = (
            product(pick_ref[1], high) + product(pick_ref[2], high) + product(pick_ref[1], low)
        ).astype(bf16)
        high, low = gathered(1)
        token_ref[...] = (product(pick_ref[0], high) + product(pick_ref[0], low)).astype(bf16)


def run_gradients(count, hidden_t, gate_grad, up_grad, inputs_t, route_grad, back, pick):
    groups = lax.axis_size("dp")
    feats, rows = inputs_t.shape
    hidden = hidden_t.shape[0]
    cap = back.shape[2]
    width = min(4 * WIDTH, hidden)
    bf16 = jnp.bfloat16

    def whole(shape):
        return pl.BlockSpec(shape, lambda i: (0,) * len(shape))

    across = pl.BlockSpec((rows, width), lambda i: (0, i))
    return pl.pallas_call(
        functools.partial(gradient_kernel, groups // EXPERTS),
        grid=(hidden // width,),
        out_shape=(
            jax.ShapeDtypeStruct((count, feats), bf16),
            jax.ShapeDtypeStruct((count, feats), bf16),
            jax.ShapeDtypeStruct((feats, hidden), bf16),
            jax.ShapeDtypeStruct((feats, hidden), bf16),
            jax.ShapeDtypeStruct((hidden, feats), bf16),
        ),
        in_specs=[
            whole((feats, rows)), across, across,
            pl.BlockSpec((width, rows), lambda i: (i, 0)),
            whole((rows, feats)), whole((2, groups, cap, feats)), whole(pick.shape),
        ],
        out_specs=(
            whole((count, feats)), whole((count, feats)),
            pl.BlockSpec((feats, width), lambda i: (0, i)),
            pl.BlockSpec((feats, width), lambda i: (0, i)),
            pl.BlockSpec((width, feats), lambda i: (i, 0)),
        ),
        compiler_params=pltpu.CompilerParams(vmem_limit_bytes=GRAD_BYTES),
    )(inputs_t, gate_grad, up_grad, hidden_t, route_grad, back, pick)


def on_device(tokens, cotangent, route_ids, gate_fixed, w_gate, w_up, w_down):
    hidden_t, gate_grad, up_grad, inputs_t, route_grad, back, pick = run_window(
        jnp.transpose(route_ids), jnp.transpose(gate_fixed), tokens, cotangent, w_gate, w_up, w_down
    )
    return run_gradients(
        tokens.shape[0], hidden_t, gate_grad, up_grad, inputs_t, route_grad, back, pick
    )


def solution(mesh):
    placed = (
        P("dp", "eshard"),
        P("dp", "eshard"),
        P("dp", None),
        P("dp", None),
        P("eshard", "dp"),
        P("eshard", "dp"),
        P("dp", "eshard"),
    )
    return jax.shard_map(
        on_device,
        mesh=mesh,
        in_specs=placed,
        out_specs=(
            P("dp", "eshard"),
            P("dp", "eshard"),
            P("eshard", "dp"),
            P("eshard", "dp"),
            P("dp", "eshard"),
        ),
        check_vma=False,
    )
```
